32 devices in a mesh: grp: 8 (over y, x, core), blk: 4 (over z).
Axes of the slice: x: 2, y: 2, z: 4, core: 2. Of those that a mesh axis runs over, the one named last changes fastest.
Arguments:
- image_tokens: bfloat16 [3, 7168, 2432], P(None, ('grp', 'blk')), may hold values from -128 to 128, as said below
- text_tokens: bfloat16 [3, 512, 2432], P(None, ('grp', 'blk')), may hold values from -128 to 128, as said below
- lengths: int32 [8], P('grp'), may hold values from 224 to 896
- image_weight: bfloat16 [2432, 2432], P('grp'), may hold values from -0.125 to 0.125
- text_weight: bfloat16 [2432, 2432], P('grp'), may hold values from -0.125 to 0.125
- gate_values: float32 [8, 2, 2432], P('grp'), may hold values from 0.5 to 2
Outputs:
- image_update: bfloat16 [7168, 2432], P(('grp', 'blk'))
- text_update: bfloat16 [512, 2432], P(('grp', 'blk'))
The draws below stay inside these ranges and needn't reach their ends.
Inputs may be any that keep to these rules, and one draw needn't show every extreme that they name: `image_tokens`: Real-valued queries, keys and values. `text_tokens`: Real-valued queries, keys and values. Request g has lengths[g] image tokens; its slots from that index up to 896 are padding, never valid keys.
All inputs are finite; a program needn't handle non-finite values.
Results may differ from the reference program's by a relative error of at most 0.0085.
Values may be sent and summed in bfloat16 or wider, within the bound.
A program may use at most 256 MiB of HBM per device.

```python
import jax
import jax.numpy as jnp
from jax import lax

HEADS = 38
HEAD_DIM = 64
D = 2432
TOK_DEV = 224
TOK_GRP = 896
GROUPS = 8
IMG = 7168
TXT = 512


def base_values(key, row_count):
    first_key = jax.random.fold_in(key, 0)
    factors = jnp.array([2.0, 1.0, 2.0], jnp.float32).reshape(3, 1, 1)
    raw = jnp.clip(jax.random.normal(first_key, (3, row_count, D), jnp.float32), -4.0, 4.0)
    return raw * factors


def draw_image_tokens(key, part):
    values = base_values(jax.random.fold_in(key, 11), IMG)
    return values.astype(jnp.bfloat16)


def draw_text_tokens(key, part):
    values = base_values(jax.random.fold_in(key, 21), TXT)
    return values.astype(jnp.bfloat16)


def place_ends(drawn, stream_key, low, largest):
    index_at = [jax.random.randint(jax.random.fold_in(stream_key, axis), (), 0, length) for axis, length in enumerate(drawn.shape)]
    main_axis = drawn.shape.index(max(drawn.shape))
    next_to = index_at[:main_axis] + [(index_at[main_axis] + 1) % drawn.shape[main_axis]] + index_at[main_axis + 1:]
    return drawn.at[tuple(index_at)].set(low).at[tuple(next_to)].set(largest)


def shard_levels(own_key, shape, cuts, least, high):
    factor_of, own = 1.0, jax.random.fold_in(own_key, 6)
    for axis_at, shards_of in cuts:
        steps = jnp.exp(jax.random.uniform(jax.random.fold_in(own, axis_at), (shards_of,), jnp.float32, least / len(cuts), high / len(cuts)))
        factor_of = factor_of * jnp.repeat(steps, shape[axis_at] // shards_of).reshape([-1 if axis == axis_at else 1 for axis in range(len(shape))])
    return factor_of


def noise(key, extent, spread, limit, cuts=(), kind=jnp.bfloat16):
    result = spread * jax.random.normal(key, extent, jnp.float32)
    if cuts:
        result = result * shard_levels(key, extent, cuts, -0.22, 0.18)
    return jnp.clip(result, -limit, limit).astype(kind)


def setup_inputs(seed: int = 0) -> dict:
    streams_of = jax.random.split(jax.random.key(seed), 7)
    image_tokens = draw_image_tokens(jax.random.fold_in(streams_of[6], 71), 0)
    text_tokens = draw_text_tokens(jax.random.fold_in(streams_of[6], 71), 0)
    lengths = place_ends(jax.random.randint(streams_of[2], (GROUPS,), TOK_DEV, TOK_GRP + 1), jax.random.fold_in(streams_of[2], 1), TOK_DEV, TOK_GRP).astype(jnp.int32)
    image_weight = noise(streams_of[3], (D, D), D ** -0.5, 0.125, ((0, 8),))
    text_weight = noise(streams_of[4], (D, D), D ** -0.5, 0.125, ((0, 8),))
    gate_values = jnp.clip(0.5 + 1.5 * jax.random.uniform(streams_of[5], (GROUPS, 2, D), jnp.float32) ** shard_levels(streams_of[5], (GROUPS, 2, D), ((0, 8),), -0.2, 0.2), 0.5, 2.0)
    return {"image_tokens": image_tokens, "text_tokens": text_tokens, "lengths": lengths, "image_weight": image_weight, "text_weight": text_weight, "gate_values": gate_values}


NEG_FILL = -1.0e30


def attend(queries, key_rows, value_rows, usable):
    query_count = queries.shape[0]
    key_count = key_rows.shape[0]
    query_heads = jnp.transpose(queries.reshape(query_count, HEADS, HEAD_DIM), (1, 0, 2))
    key_heads = jnp.transpose(key_rows.reshape(key_count, HEADS, HEAD_DIM), (1, 0, 2))
    value_heads = jnp.transpose(value_rows.reshape(key_count, HEADS, HEAD_DIM), (1, 0, 2))

    def one_head(inputs):
        query_head, key_head, value_head = inputs
        scores = jnp.dot(query_head, key_head.T, preferred_element_type=jnp.float32) * (HEAD_DIM ** -0.5)
        scores = jnp.where(usable[None, :], scores, NEG_FILL)
        row_max = jnp.max(scores, axis=1, keepdims=True)
        probs = jnp.where(usable[None, :], jnp.exp(scores - row_max), 0.0)
        totals = jnp.sum(probs, axis=1, keepdims=True)
        summed = jnp.dot(probs.astype(jnp.bfloat16), value_head, preferred_element_type=jnp.float32)
        return summed / totals

    outputs = lax.map(one_head, (query_heads, key_heads, value_heads))
    merged = jnp.transpose(outputs, (1, 0, 2)).reshape(query_count, HEADS * HEAD_DIM)
    return merged.astype(jnp.bfloat16)


def reference(image_tokens, text_tokens, lengths, image_weight, text_weight, gate_values):
    group_count = lengths.shape[0]
    model_width = image_tokens.shape[2]
    image_rows = image_tokens.shape[1] // group_count
    text_rows = text_tokens.shape[1] // group_count
    image_groups = jnp.transpose(image_tokens.reshape(3, group_count, image_rows, model_width), (1, 0, 2, 3))
    text_groups = jnp.transpose(text_tokens.reshape(3, group_count, text_rows, model_width), (1, 0, 2, 3))

    def one_group(inputs):
        image_part, text_part, length, gates = inputs
        queries = jnp.concatenate([image_part[0], text_part[0]], axis=0)
        key_rows = jnp.concatenate([image_part[1], text_part[1]], axis=0)
        value_rows = jnp.concatenate([image_part[2], text_part[2]], axis=0)
        usable = jnp.concatenate([jnp.arange(image_rows, dtype=jnp.int32) < length,
                                  jnp.ones((text_rows,), dtype=jnp.bool_)], axis=0)
        attended = attend(queries, key_rows, value_rows, usable)
        image_out = jnp.dot(attended[:image_rows], image_weight, preferred_element_type=jnp.float32) * gates[0]
        text_out = jnp.dot(attended[image_rows:], text_weight, preferred_element_type=jnp.float32) * gates[1]
        return image_out.astype(jnp.bfloat16), text_out.astype(jnp.bfloat16)

    image_out, text_out = lax.map(one_group, (image_groups, text_groups, lengths, gate_values))
    return image_out.reshape(-1, model_width), text_out.reshape(-1, model_width)
```

```python
import functools

import jax
import jax.numpy as jnp
from jax import lax
from jax.experimental import pallas as pl
from jax.experimental.pallas import tpu as pltpu
from jax.sharding import PartitionSpec as P

HEADS = 38
NEG_FILL = -1e30
LANES = 128
MESH = pl.DeviceIdType.MESH


def key_mask(row_count, image_rows, text_rows, length):
    row_ids = jnp.arange(row_count, dtype=jnp.int32)
    shard_span = image_rows + text_rows
    shard_idx = row_ids // shard_span
    within = row_ids % shard_span
    return (within >= image_rows) | (shard_idx * image_rows + within < length)


def exchange_kernel(
    n, head_size,
    img, txt, bias, out_img, out_txt,
    qkv, done_img, done_txt,
    in_send, in_recv, in_local, out_send, out_recv, out_local,
):
    me = lax.axis_index("blk")
    image_rows, text_rows = img.shape[1], txt.shape[1]
    span = image_rows + text_rows
    pairs = img.shape[2] // LANES
    base, extra = divmod(pairs, n)
    most = qkv.shape[0]

    def count(b):
        return base + jnp.where(b < extra, 1, 0)

    def columns(b, p):
        return pl.ds(pl.multiple_of((b * base + jnp.minimum(b, extra) + p) * LANES, LANES), LANES)

    def image_slot(p, b):
        return qkv.at[p, :, pl.ds(pl.multiple_of(b * span, 16), image_rows), :]

    def text_slot(p, b):
        return qkv.at[p, :, pl.ds(pl.multiple_of(b * span + image_rows, 16), text_rows), :]

    barrier = pltpu.get_barrier_semaphore()
    for d in range(1, n):
        pl.semaphore_signal(barrier, inc=1, device_id={"blk": lax.rem(me + d, n)}, device_id_type=MESH)
    pl.semaphore_wait(barrier, n - 1)

    def in_copies(p, dest, owner, d):
        cols = columns(dest, p)
        return [
            pltpu.make_async_remote_copy(
                src_ref=src.at[:, :, cols], dst_ref=slot(p, owner),
                send_sem=in_send.at[p, d, i], recv_sem=in_recv.at[p, owner, i],
                device_id={"blk": dest}, device_id_type=MESH)
            for i, (src, slot) in enumerate(((img, image_slot), (txt, text_slot)))
        ]

    def own_copies(p):
        cols = columns(me, p)
        return [
            pltpu.make_async_copy(src.at[:, :, cols], slot(p, me), in_local.at[p, i])
            for i, (src, slot) in enumerate(((img, image_slot), (txt, text_slot)))
        ]

    def image_out(p, dest, owner, d):
        return pltpu.make_async_remote_copy(
            src_ref=done_img.at[p, dest], dst_ref=out_img.at[:, columns(owner, p)],
            send_sem=out_send.at[p, d, 0], recv_sem=out_recv.at[p, owner, 0],
            device_id={"blk": dest}, device_id_type=MESH)

    def text_out(p, dest, owner, d):
        return pltpu.make_async_remote_copy(
            src_ref=done_txt.at[p], dst_ref=out_txt.at[:, columns(owner, p)],
            send_sem=out_send.at[p, d, 1], recv_sem=out_recv.at[p, owner, 1],
            device_id={"blk": dest}, device_id_type=MESH)

    def image_own(p):
        return pltpu.make_async_copy(done_img.at[p, me], out_img.at[:, columns(me, p)], out_local.at[p, 0])

    def text_own(p):
        return pltpu.make_async_copy(done_txt.at[p], out_txt.at[:, columns(me, p)], out_local.at[p, 1])

    for p in range(most):
        for d in range(1, n):
            dest = lax.rem(me + d, n)

            @pl.when(p < count(dest))
            def _():
                for copy in in_copies(p, dest, me, d):
                    copy.start()

        @pl.when(p < count(me))
        def _():
            for copy in own_copies(p):
                copy.start()

    first = lax.broadcasted_iota(jnp.int32, (span, LANES), 1) < head_size
    scale = head_size ** (-0.5)

    def one_pair(p, _):
        for copy in own_copies(p):
            copy.wait()
        for d in range(1, n):
            for copy in in_copies(p, me, lax.rem(me + d, n), d):
                copy.wait_recv()

        def one_block(j, _):
            dest = lax.rem(me + 1 + j, n)
            rows = pl.ds(pl.multiple_of(dest * span, 16), span)
            queries = qkv[p, 0, rows, :]
            halves = []
            for h in range(2):
                own = first if h == 0 else jnp.logical_not(first)
                q_h = jnp.where(own, queries, jnp.zeros_like(queries))
                scores = lax.dot_general(
                    q_h, qkv[p, 1], (((1,), (1,)), ((), ())), preferred_element_type=jnp.float32
                ) * scale + bias[...]
                weights = jnp.exp(scores - jnp.max(scores, axis=1, keepdims=True))
                totals = jnp.sum(weights, axis=1, keepdims=True)
                summed = jnp.dot(weights.astype(jnp.bfloat16), qkv[p, 2], preferred_element_type=jnp.float32)
                halves.append(summed / totals)
            out = jnp.where(first, halves[0], halves[1]).astype(jnp.bfloat16)
            done_img[p, dest] = out[:image_rows]
            done_txt[p, pl.ds(pl.multiple_of(dest * text_rows, 16), text_rows), :] = out[image_rows:]

            @pl.when(j < n - 1)
            def _():
                image_out(p, dest, me, j + 1).start()

            return 0

        lax.fori_loop(0, n, one_block, 0)
        image_own(p).start()
        text_own(p).start()
        for d in range(1, n):
            text_out(p, lax.rem(me + d, n), me, d).start()
        return 0

    lax.fori_loop(0, count(me), one_pair, 0)

    for p in range(most):
        for d in range(1, n):
            peer = lax.rem(me + d, n)

            @pl.when(p < count(peer))
            def _():
                for copy in in_copies(p, peer, me, d):
                    copy.wait_send()
                image_out(p, me, peer, d).wait_recv()
                text_out(p, me, peer, d).wait_recv()

            @pl.when(p < count(me))
            def _():
                image_out(p, peer, me, d).wait_send()
                text_out(p, peer, me, d).wait_send()

        @pl.when(p < count(me))
        def _():
            image_own(p).wait()
            text_own(p).wait()


def attend(image_tokens, text_tokens, bias, n, head_size):
    image_rows, text_rows, width = image_tokens.shape[1], text_tokens.shape[1], image_tokens.shape[2]
    span = image_rows + text_rows
    most = -(-(width // LANES) // n)
    dma = pltpu.SemaphoreType.DMA
    any_space = pl.BlockSpec(memory_space=pl.ANY)
    return pl.pallas_call(
        functools.partial(exchange_kernel, n, head_size),
        out_shape=(
            jax.ShapeDtypeStruct((image_rows, width), jnp.bfloat16),
            jax.ShapeDtypeStruct((n * text_rows, width), jnp.bfloat16),
        ),
        in_specs=[any_space, any_space, pl.BlockSpec(memory_space=pltpu.VMEM)],
        out_specs=(any_space, any_space),
        scratch_shapes=[
            pltpu.VMEM((most, 3, n * span, LANES), jnp.bfloat16),
            pltpu.VMEM((most, n, image_rows, LANES), jnp.bfloat16),
            pltpu.VMEM((most, n * text_rows, LANES), jnp.bfloat16),
            dma((most, n, 2)), dma((most, n, 2)), dma((most, 2)),
            dma((most, n, 2)), dma((most, n, 2)), dma((most, 2)),
        ],
        compiler_params=pltpu.CompilerParams(
            collective_id=0, has_side_effects=True, vmem_limit_bytes=48 * 1024 * 1024
        ),
        name="attend",
    )(image_tokens, text_tokens, bias)


def per_device(image_tokens, text_tokens, lengths, image_weight, text_weight, gate_values):
    image_rows = image_tokens.shape[1]
    text_rows = text_tokens.shape[1]
    width = image_tokens.shape[2]
    n = lax.axis_size("blk")
    me = lax.axis_index("blk")
    share = width // n
    usable = key_mask((image_rows + text_rows) * n, image_rows, text_rows, lengths[0])
    bias = jnp.where(usable, 0.0, NEG_FILL).astype(jnp.float32)[None, :]
    own_text = lax.dynamic_slice_in_dim(text_weight, me * share, share, axis=1)
    image_full = lax.all_gather(image_weight, "grp", axis=0, tiled=True)
    text_full = lax.all_gather(own_text, "grp", axis=0, tiled=True)
    image_attended, text_attended = attend(image_tokens, text_tokens, bias, n, width // HEADS)
    text_gate = lax.dynamic_slice_in_dim(gate_values[0, 1], me * share, share, axis=0)
    text_part = (
        jnp.dot(text_attended, text_full, preferred_element_type=jnp.float32) * text_gate
    ).astype(jnp.bfloat16)
    text_update = lax.all_to_all(text_part, "blk", split_axis=0, concat_axis=1, tiled=True)
    image_update = (
        jnp.dot(image_attended, image_full, preferred_element_type=jnp.float32) * gate_values[0, 0]
    ).astype(jnp.bfloat16)
    return (image_update, text_update)


def solution(mesh):
    in_specs = (
        P(None, ("grp", "blk"), None),
        P(None, ("grp", "blk"), None),
        P("grp"),
        P("grp", None),
        P("grp", None),
        P("grp", None, None),
    )
    out_specs = (P(("grp", "blk"), None), P(("grp", "blk"), None))
    return jax.shard_map(
        per_device, mesh=mesh, in_specs=in_specs, out_specs=out_specs, check_vma=False
    )
```
